32 devices in a mesh: row: 8 (over z, x), col: 4 (over y, core).
Axes of the slice: x: 2, y: 2, z: 4, core: 2. Of those that a mesh axis runs over, the one named last changes fastest.
Arguments:
- panel: float32 [2560, 256], P('row', 'col'), may hold values from 0 to 65520, as said below
- trail: float32 [2560, 16384], P('row', 'col'), may hold values from 0 to 65520, as said below
- leaf_pick: int32 [8, 256], P('row'), may hold values from 0 to 319, as said below
- node_pick: int32 [7, 256], replicated, may hold values from 0 to 511, as said below
Outputs:
- schur: float32 [2560, 16384], P('row', 'col')
- multipliers: float32 [2560, 256], P('row')
The draws below stay inside these ranges and needn't reach their ends.
Inputs may be any that keep to these rules, and one draw needn't show every extreme that they name: `leaf_pick`: each row holds 256 different local row numbers. `node_pick`: each row holds 256 different positions among the node's 2 * 256 candidates. Entries are whole residues; the panel rows of pivot_ids, in that order, form a unit upper-triangular matrix modulo 65521. `trail`: entries are whole residues.
All inputs are finite; a program needn't handle non-finite values.
Results may differ from the reference program's by a relative error of at most 0.0003.
Values sent between devices are 32-bit elements; how exact they have to be, the bound alone decides.
No kernel may reach another device: no remote copies, remote signals or barrier semaphores. Data moves between devices by JAX's collectives and lax.ppermute only.
A program may use at most 128 MiB of HBM per device.

```python
import jax
import jax.numpy as jnp
from jax import lax

W = 256
RD = 320
ROWS = 2560
COLS = 16384
N_ROW = 8


def pick_tables(key):
    leaf_keys = jax.random.split(jax.random.fold_in(key, 11), N_ROW)
    node_keys = jax.random.split(jax.random.fold_in(key, 12), N_ROW - 1)
    leaf_table = jax.vmap(lambda one_key: jax.random.permutation(one_key, RD)[:W])(leaf_keys)
    node_table = jax.vmap(lambda one_key: jax.random.permutation(one_key, 2 * W)[:W])(node_keys)
    return (leaf_table.astype(jnp.int32), node_table.astype(jnp.int32))


def tree_roots(leaf_table, node_table):
    branch_ids = jnp.zeros((W,), jnp.int32)
    position = jnp.arange(W, dtype=jnp.int32)
    depth_count = N_ROW.bit_length() - 1
    for height in reversed(range(depth_count)):
        offset = N_ROW - (N_ROW >> height)
        picked = node_table[offset + branch_ids, position]
        branch_ids = 2 * branch_ids + picked // W
        position = picked % W
    return branch_ids * RD + leaf_table[branch_ids, position]


def draw_leaf_pick(key, part):
    return pick_tables(key)[0]


def draw_node_pick(key, part):
    return pick_tables(key)[1]


def draw_panel(key, part):
    base_values = jax.random.randint(jax.random.fold_in(key, 21), (ROWS, W), 0, 65521)
    leaf_table, node_table = pick_tables(key)
    pivot_ids = tree_roots(leaf_table, node_table)
    above = jax.random.randint(jax.random.fold_in(key, 22), (W, W), 0, 65521)
    row_index = jnp.arange(W, dtype=jnp.int32)[:, None]
    col_index = jnp.arange(W, dtype=jnp.int32)[None, :]
    triangle = jnp.where(col_index > row_index, above, jnp.where(col_index == row_index, 1, 0))
    return base_values.at[pivot_ids].set(triangle).astype(jnp.float32)


def draw_trail(key, part):
    return jax.random.randint(jax.random.fold_in(key, 31), (ROWS, COLS), 0, 65521).astype(jnp.float32)


def setup_inputs(seed: int = 0) -> dict:
    splits = jax.random.split(jax.random.key(seed), 5)
    panel = draw_panel(jax.random.fold_in(splits[4], 71), 0)
    trail = draw_trail(jax.random.fold_in(splits[4], 71), 0)
    leaf_pick = draw_leaf_pick(jax.random.fold_in(splits[4], 71), 0)
    node_pick = draw_node_pick(jax.random.fold_in(splits[4], 71), 0)
    return {"panel": panel, "trail": trail, "leaf_pick": leaf_pick, "node_pick": node_pick}


MODULUS = 65521.0


def residue(values):
    return jnp.mod(values, MODULUS)


def limbs(values):
    upper_limb = jnp.floor(values / 256.0)
    lower_limb = values - 256.0 * upper_limb
    return upper_limb.astype(jnp.bfloat16), lower_limb.astype(jnp.bfloat16)


def modmul(first_factor, second_factor):
    first_upper, first_lower = limbs(first_factor)
    second_upper, second_lower = limbs(second_factor)
    high_part = residue(jnp.dot(first_upper, second_upper, preferred_element_type=jnp.float32))
    cross_one = residue(jnp.dot(first_upper, second_lower, preferred_element_type=jnp.float32))
    cross_two = residue(jnp.dot(first_lower, second_upper, preferred_element_type=jnp.float32))
    low_part = residue(jnp.dot(first_lower, second_lower, preferred_element_type=jnp.float32))
    middle = residue(cross_one + cross_two)
    return residue(residue(15.0 * high_part) + residue(256.0 * middle) + low_part)


def invert_unit(pivot_block):
    width = pivot_block.shape[0]
    identity = jnp.eye(width, dtype=jnp.float32)
    nilpotent = pivot_block - identity
    inverse = residue(identity - nilpotent + MODULUS)
    power = nilpotent
    for section in range((width - 1).bit_length() - 1):
        power = modmul(power, power)
        inverse = modmul(inverse, residue(identity + power))
    return inverse


def root_ids(leaf_pick, node_pick):
    branch_ids = jnp.zeros((W,), jnp.int32)
    position = jnp.arange(W, dtype=jnp.int32)
    depth_count = N_ROW.bit_length() - 1
    for height in reversed(range(depth_count)):
        offset = N_ROW - (N_ROW >> height)
        picked = node_pick[offset + branch_ids, position]
        branch_ids = 2 * branch_ids + picked // W
        position = picked % W
    return branch_ids * RD + leaf_pick[branch_ids, position]


def reference(panel, trail, leaf_pick, node_pick):
    pivot_ids = root_ids(leaf_pick, node_pick)
    pivot_block = panel[pivot_ids]
    pivot_trail = trail[pivot_ids]
    inverse = invert_unit(pivot_block)
    factors = modmul(panel, inverse)
    trail_blocks = trail.reshape(N_ROW, RD, COLS)
    factor_blocks = factors.reshape(N_ROW, RD, W)

    def update(pair):
        trail_block, factor_block = pair
        return residue(trail_block + (MODULUS - modmul(factor_block, pivot_trail)))

    remainder = lax.map(update, (trail_blocks, factor_blocks)).reshape(ROWS, COLS)
    return remainder / MODULUS, factors / MODULUS
```

```python
import functools

import jax
import jax.numpy as jnp
from jax import lax
from jax.experimental import pallas as pl
from jax.experimental.pallas import tpu as pltpu
from jax.sharding import PartitionSpec as P

MODULUS = 65521.0
INVERSE = 1.0 / MODULUS
F32 = jnp.float32
BF16 = jnp.bfloat16
I32 = jnp.int32
VMEM = pltpu.MemorySpace.VMEM
SMEM = pltpu.MemorySpace.SMEM
NT = (((1,), (1,)), ((), ()))
TN = (((0,), (0,)), ((), ()))
NN = (((1,), (0,)), ((), ()))


def dot(a, b, dims=NN):
    return lax.dot_general(a, b, dims, preferred_element_type=F32)


def iota(shape, axis):
    return lax.broadcasted_iota(I32, shape, axis)


def ones_where(mask):
    return jnp.where(mask, 1.0, 0.0).astype(BF16)


def high_low(values):
    upper = jnp.floor(values * (1.0 / 256.0))
    return upper.astype(BF16), (values - 256.0 * upper).astype(BF16)


def centred_limbs(values):
    upper = jnp.round(values * (1.0 / 256.0))
    return upper.astype(BF16), (values - 256.0 * upper).astype(BF16)


def centred(values):
    return values - MODULUS * jnp.round(values * INVERSE)


def centred_256(values):
    quotient = jnp.round(values * (256.0 * INVERSE))
    return 256.0 * (values - 256.0 * quotient) + 15.0 * quotient


def left_limbs(values):
    f_upper, f_lower = centred_limbs(values)
    g_upper, g_lower = centred_limbs(centred_256(values))
    upper = jnp.concatenate([g_upper, f_upper], axis=1)
    lower = jnp.concatenate([g_lower, f_lower], axis=1)
    return jnp.concatenate([upper, lower], axis=0)


def right_limbs(values):
    upper, lower = centred_limbs(values)
    return jnp.concatenate([upper, lower], axis=0)


def product(left, right):
    count = left.shape[0]
    both = dot(left_limbs(left), right_limbs(right))
    return centred_256(both[:count]) + both[count:]


def find_kernel(
    devices, first, more, place_ref, node_ref, leaf_ref, panel_ref, trail_ref,
    lower_ref, upper_ref, extra_ref, block_ref, info_ref, most_ref,
    staged, rows, staged_sem, row_sem,
):
    width = node_ref.shape[1]
    row_count = panel_ref.shape[0]
    half = lower_ref.shape[1]
    slots = first + more
    place = place_ref[0]

    nodes = node_ref[...]
    node_upper = nodes >= width
    node_high = ones_where(node_upper)
    node_low = jnp.where(node_upper, nodes - width, nodes).astype(F32).astype(BF16)
    node_index = iota(nodes.shape, 0)
    leaf_high, leaf_low = high_low(leaf_ref[...].astype(F32))

    square = (width, width)
    branch = jnp.zeros((1, width), I32)
    position = iota((1, width), 1)
    for height in reversed(range(devices.bit_length() - 1)):
        offset = devices - (devices >> height)
        hit = ones_where(iota(square, 0) == position)
        chosen = node_index == branch + offset
        high = jnp.sum(jnp.where(chosen, dot(node_high, hit), 0.0), axis=0, keepdims=True)
        low = jnp.sum(jnp.where(chosen, dot(node_low, hit), 0.0), axis=0, keepdims=True)
        branch = 2 * branch + high.astype(I32)
        position = low.astype(I32)
    hit = ones_where(iota(square, 0) == position)
    row_high = dot(leaf_high, hit)
    row_low = dot(leaf_low, hit)

    padded = max(devices, 8)
    owned_by = iota((padded, width), 0) == branch
    earlier = ones_where(iota(square, 0) < iota(square, 1))
    before = dot(ones_where(owned_by), earlier)
    rank = jnp.sum(jnp.where(owned_by, before, 0.0), axis=0, keepdims=True).astype(I32)
    most_ref[0, 0] = jnp.max(rank) + 1
    info_ref[0:1, :] = branch
    info_ref[1:2, :] = rank

    key = jnp.where(branch == place, rank, -1)
    mine = iota((slots, width), 0) == key
    mine_ones = ones_where(mine)
    slot_rows = 256.0 * dot(row_high.astype(BF16), mine_ones, NT) + dot(
        row_low.astype(BF16), mine_ones, NT
    )
    staged[0:1, 0:slots] = jnp.clip(slot_rows.astype(I32), 0, row_count - 1)
    to_scalar = pltpu.make_async_copy(staged, rows, staged_sem)
    to_scalar.start()
    to_scalar.wait()

    def copies(slot):
        row = pl.ds(rows[0, slot], 1)
        if slot < first:
            here = pl.ds(slot, 1)
            return [
                pltpu.make_async_copy(
                    trail_ref.at[row, pl.ds(0, half)], lower_ref.at[here, :], row_sem
                ),
                pltpu.make_async_copy(
                    trail_ref.at[row, pl.ds(half, half)], upper_ref.at[here, :], row_sem
                ),
            ]
        here = pl.ds(slot - first, 1)
        return [
            pltpu.make_async_copy(trail_ref.at[row, :], extra_ref.at[here, :], row_sem)
        ]

    started = [copy for slot in range(slots) for copy in copies(slot)]
    for copy in started:
        copy.start()

    row_values = 256.0 * row_high + row_low
    slot_column = jnp.sum(jnp.where(mine, row_values, 0.0), axis=1, keepdims=True)
    picker = ones_where(iota((slots, row_count), 1) == slot_column.astype(I32))
    panel_high, panel_low = high_low(panel_ref[...])
    block_ref[...] = 256.0 * dot(picker, panel_high) + dot(picker, panel_low)

    for copy in started:
        copy.wait()


def find_pivots(place, node_pick, leaf_pick, panel, trail, devices, first, more):
    width = node_pick.shape[1]
    row_count, part_width = panel.shape
    columns = trail.shape[1]
    half = columns // 2
    lanes = -(-(first + more) // 128) * 128
    whole = pl.BlockSpec(memory_space=VMEM)
    return pl.pallas_call(
        functools.partial(find_kernel, devices, first, more),
        out_shape=(
            jax.ShapeDtypeStruct((first, half), F32),
            jax.ShapeDtypeStruct((first, half), F32),
            jax.ShapeDtypeStruct((more, columns), F32),
            jax.ShapeDtypeStruct((first + more, part_width), F32),
            jax.ShapeDtypeStruct((8, width), I32),
            jax.ShapeDtypeStruct((1, 1), I32),
        ),
        in_specs=[
            pl.BlockSpec(memory_space=SMEM), whole, whole, whole,
            pl.BlockSpec(memory_space=pl.ANY),
        ],
        out_specs=(whole, whole, whole, whole, whole, pl.BlockSpec(memory_space=SMEM)),
        scratch_shapes=[
            pltpu.VMEM((8, lanes), I32),
            pltpu.SMEM((8, lanes), I32),
            pltpu.SemaphoreType.DMA,
            pltpu.SemaphoreType.DMA,
        ],
        compiler_params=pltpu.CompilerParams(vmem_limit_bytes=24 << 20),
        name="find_pivots",
    )(place, node_pick, leaf_pick, panel, trail)


def ring_place(index, devices):
    return jnp.where(index % 2 == 0, index // 2, devices - 1 - index // 2)


def factor_kernel(
    devices, slots, unit, parts, place_ref, info_ref, gathered_ref,
    multiplier_ref, limbs_ref, shift_ref,
):
    width = info_ref.shape[1]
    total = devices * slots
    place = place_ref[0]
    column = place_ref[1]
    owner = info_ref[0:1, :]
    rank = info_ref[1:2, :]

    part_width = width // parts
    source = iota((width, width), 0)
    target = (source // part_width ^ column) * part_width + source % part_width
    reorder = ones_where(target == iota((width, width), 1))
    high, low = high_low(gathered_ref[...])
    high = dot(high, reorder)
    low = dot(low, reorder)

    slot = slots * (owner ^ place) + rank
    picker = ones_where(iota((total, width), 0) == slot)
    block = 256.0 * dot(picker, high[:total].astype(BF16), TN) + dot(
        picker, low[:total].astype(BF16), TN
    )
    panel = centred(256.0 * high[total:] + low[total:])
    diagonal = iota((width, width), 0) == iota((width, width), 1)
    power = centred(block - jnp.where(diagonal, 1.0, 0.0))

    last = (width - 1).bit_length() - 1
    for section in range(last + 1):
        if section < last:
            both = product(jnp.concatenate([power, panel], axis=0), power)
            change = both[width:]
        else:
            change = product(panel, power)
        panel = centred(panel - change if section == 0 else panel + change)
        if section < last:
            power = centred(both[:width])

    multiplier_ref[...] = jnp.where(panel < 0.0, panel + MODULUS, panel) / MODULUS

    shift = centred_256(jnp.sum(panel, axis=1, keepdims=True))
    quotient = jnp.round(shift * (128.0 * INVERSE))
    shift = 128.0 * (shift - 512.0 * quotient) + 15.0 * quotient
    shift_ref[...] = jnp.broadcast_to(shift - 0.5, shift_ref.shape)

    if unit:
        behind = ring_place(place, devices) - ring_place(owner, devices)
        behind = jnp.where(behind < 0, behind + devices, behind)
        arrival = unit * behind + rank
        depth = unit * devices
        twice = jnp.concatenate([arrival, arrival + depth], axis=1)
        order = ones_where(iota((2 * depth, 2 * width), 0) == twice)
        limbs_ref[...] = dot(left_limbs(panel), order, NT).astype(BF16)
    else:
        limbs_ref[...] = left_limbs(panel)


def find_factors(places, info, gathered, devices, slots, unit, parts):
    width = info.shape[1]
    row_count = gathered.shape[0] - devices * slots
    depth = unit * devices if unit else width
    whole = pl.BlockSpec(memory_space=VMEM)
    return pl.pallas_call(
        functools.partial(factor_kernel, devices, slots, unit, parts),
        out_shape=(
            jax.ShapeDtypeStruct((row_count, width), F32),
            jax.ShapeDtypeStruct((2 * row_count, 2 * depth), BF16),
            jax.ShapeDtypeStruct((row_count, 128), F32),
        ),
        in_specs=[pl.BlockSpec(memory_space=SMEM), whole, whole],
        out_specs=(whole, whole, whole),
        compiler_params=pltpu.CompilerParams(vmem_limit_bytes=48 << 20),
        cost_estimate=pl.CostEstimate(
            flops=20_000_000_000, bytes_accessed=4_000_000, transcendentals=0
        ),
        name="find_factors",
    )(places, info, gathered)


def update_kernel(count, limbs_ref, shift_ref, trail_ref, *refs):
    pieces = refs[:count]
    out_ref = refs[-1]
    rows, columns = trail_ref.shape
    values = jnp.concatenate([piece[...] for piece in pieces], axis=0)
    upper = jnp.round(values * (1.0 / 256.0))
    lower = values - 256.0 * upper
    right = jnp.concatenate([(upper - 128.0).astype(BF16), lower.astype(BF16)], axis=0)
    both = dot(limbs_ref[...], right)
    high, low = both[:rows], both[rows:]
    quotient = jnp.round((256.0 * high + low) * INVERSE)
    rest = 256.0 * (high - 256.0 * quotient) + (low + 15.0 * quotient)
    shift = jnp.concatenate([shift_ref[...]] * (columns // 128), axis=1)
    ratio = (trail_ref[...] - shift - rest) * INVERSE
    out_ref[...] = (ratio - 0.5 * INVERSE) - jnp.floor(ratio)


def update(limbs, shift, trail, pieces, first_column, columns, before):
    rows, total = trail.shape
    step = 256
    first = first_column // step
    depth = sum(piece.shape[0] for piece in pieces)

    def fixed(array):
        return pl.BlockSpec(array.shape, lambda i: (0, 0), pipeline_mode=pl.Buffered(1))

    in_specs = [
        fixed(limbs), fixed(shift), pl.BlockSpec((rows, step), lambda i: (0, first + i))
    ]
    in_specs += [pl.BlockSpec((piece.shape[0], step), lambda i: (0, i)) for piece in pieces]
    operands = [limbs, shift, trail, *pieces]
    aliases = {}
    if before is not None:
        in_specs.append(pl.BlockSpec(memory_space=pl.ANY))
        aliases = {len(operands): 0}
        operands.append(before)
    return pl.pallas_call(
        functools.partial(update_kernel, len(pieces)),
        out_shape=jax.ShapeDtypeStruct((rows, total), F32),
        grid=(columns // step,),
        in_specs=in_specs,
        out_specs=pl.BlockSpec((rows, step), lambda i: (0, first + i)),
        input_output_aliases=aliases,
        compiler_params=pltpu.CompilerParams(vmem_limit_bytes=24 << 20),
        cost_estimate=pl.CostEstimate(
            flops=8 * rows * depth * columns,
            bytes_accessed=4 * columns * (2 * rows + depth),
            transcendentals=0,
        ),
        name="update",
    )(*operands)


def swapped(block, axis, bit):
    count = lax.axis_size(axis)
    return lax.ppermute(block, axis, [(place, place ^ 1 << bit) for place in range(count)])


def ring_gather(lower, upper, axis):
    count = lax.axis_size(axis)
    order = list(range(0, count, 2)) + list(range(count - 1, 0, -2))
    ahead = [(order[k], order[(k + 1) % count]) for k in range(count)]
    back = [(there, here) for here, there in ahead]
    found = [{0: lower}, {0: upper}]
    for step in range(1, count // 2 + 1):
        for part in (0, 1):
            held = found[part]
            if step < count // 2 or part == 0:
                held[step] = lax.ppermute(held[step - 1], axis, ahead)
            if step < count // 2 or part == 1:
                source = held[(count - step + 1) % count]
                held[count - step] = lax.ppermute(source, axis, back)
    return [[held[k] for k in range(count)] for held in found]


def per_device(panel, trail, leaf_pick, node_pick):
    width = leaf_pick.shape[1]
    columns = trail.shape[1]
    half = columns // 2
    devices = lax.axis_size("row")
    parts = lax.axis_size("col")
    depth_count = devices.bit_length() - 1
    first = width // devices // 8 * 8 + 8
    more = 8
    place = lax.axis_index("row").astype(I32)
    places = jnp.stack([place, lax.axis_index("col").astype(I32)])
    lower, upper, extra, block, info, most = find_pivots(
        places, node_pick, leaf_pick, panel, trail, devices, first, more
    )

    def gather_panel():
        rows = block
        for bit in range(depth_count):
            rows = jnp.concatenate([rows, swapped(rows, "row", bit)], axis=0)
        both = jnp.concatenate([rows, panel], axis=0)
        for bit in range(parts.bit_length() - 1):
            both = jnp.concatenate([both, swapped(both, "col", bit)], axis=1)
        return both

    def by_ring(unit):
        if unit == first:
            low_unit, high_unit = lower, upper
        else:
            low_unit = jnp.concatenate([lower, extra[:, :half]], axis=0)
            high_unit = jnp.concatenate([upper, extra[:, half:]], axis=0)
        low_units, high_units = ring_gather(low_unit, high_unit, "row")
        multipliers, limbs, shift = find_factors(
            places, info, gather_panel(), devices, first + more, unit, parts
        )
        schur = update(limbs, shift, trail, low_units, 0, half, None)
        schur = update(limbs, shift, trail, high_units, half, half, schur)
        return schur, multipliers

    def in_general():
        owner, rank = info[0], info[1]
        own_rows = jnp.zeros((width,), I32)
        branch, position = jnp.zeros((width,), I32), jnp.arange(width, dtype=I32)
        for height in reversed(range(depth_count)):
            picked = node_pick[devices - (devices >> height) + branch, position]
            branch, position = 2 * branch + picked // width, picked % width
        own_rows = leaf_pick[0][position]
        owned = (owner == place)[:, None]
        rows = jnp.where(owned, trail[own_rows], 0.0)
        wide = jnp.where(owned, panel[own_rows], 0.0)
        for bit in range(depth_count):
            rows = rows + swapped(rows, "row", bit)
            wide = wide + swapped(wide, "row", bit)
        both = jnp.concatenate([wide, panel], axis=0)
        for bit in range(parts.bit_length() - 1):
            both = jnp.concatenate([both, swapped(both, "col", bit)], axis=1)
        natural = jnp.zeros_like(info).at[1].set(jnp.arange(width, dtype=I32))
        natural = natural.at[0].set(place)
        multipliers, limbs, shift = find_factors(
            places, natural, both, 1, width, 0, parts
        )
        schur = update(limbs, shift, trail, [rows], 0, columns, None)
        return schur, multipliers

    level = jnp.where(most[0, 0] <= first, 0, jnp.where(most[0, 0] <= first + more, 1, 2))
    return lax.switch(
        level,
        [functools.partial(by_ring, first), functools.partial(by_ring, first + more), in_general],
    )


def solution(mesh):
    in_specs = (P("row", "col"), P("row", "col"), P("row", None), P())
    out_specs = (P("row", "col"), P("row", None))
    return jax.shard_map(
        per_device, mesh=mesh, in_specs=in_specs, out_specs=out_specs, check_vma=False
    )
```
